256 devices in a mesh: ctx: 16 (over z, x_hi), fsdp: 16 (over x_lo, y, core).
Axes of the slice: x: 4 (x_hi: 2, x_lo: 2; x = x_hi * 2 + x_lo), y: 4, z: 8, core: 2. Of those that a mesh axis runs over, the one named last changes fastest.
Arguments:
- out_grad: bfloat16 [2048, 8192], P('ctx', 'fsdp'), may hold values from -6 to 6
- out_weight: bfloat16 [8192, 8192], P('ctx', 'fsdp'), may hold values from -0.0625 to 0.0625
- projections: bfloat16 [3, 2048, 8192], P(None, 'ctx', 'fsdp'), may hold values from -6 to 6
- short_filters: float32 [3, 3, 8192], P(None, None, 'fsdp'), may hold values from -3 to 3
- residues: float32 [16, 8192], P(None, 'fsdp'), may hold values from -0.06 to 0.06
- decay_rates: float32 [16, 8192], P(None, 'fsdp'), may hold values from 4.8828126e-05 to 0.05
Outputs:
- grad_weight: bfloat16 [8192, 8192], P('ctx', 'fsdp')
- grad_projections: bfloat16 [3, 2048, 8192], P(None, 'ctx', 'fsdp')
- grad_short: float32 [3, 3, 8192], P(None, None, 'fsdp')
- grad_residues: float32 [16, 8192], P(None, 'fsdp')
- grad_rates: float32 [16, 8192], P(None, 'fsdp')
The draws below stay inside these ranges and needn't reach their ends.
All inputs are finite; a program needn't handle non-finite values.
Results may differ from the reference program's by a relative error of at most 0.005.
Values may be sent and summed in bfloat16 or wider, within the bound.
No kernel may reach another device: no remote copies, remote signals or barrier semaphores. Data moves between devices by JAX's collectives and lax.ppermute only.
A program may use at most 128 MiB of HBM per device.

```python
import math
import jax
import jax.numpy as jnp
from jax import lax

D = 8192
SHORT = 3
N_MODES = 16
TOKENS = 2048


def strengthened(values, rng, source, target, blocks, factor):
    def block_of(dim):
        return (jnp.arange(values.shape[dim]) // (values.shape[dim] // blocks)).reshape((-1,) + (1,) * (values.ndim - 1 - dim))

    first = jax.random.permutation(rng, blocks)[block_of(target)]
    second = (block_of(target) + blocks // 2) % blocks
    return jnp.where((block_of(source) == first) | (block_of(source) == second), factor * values, values)


def levels(own_key, extent, cuts, least, largest):
    loudness = 1.0
    for dim, shards_of in cuts:
        draws = jax.random.uniform(jax.random.fold_in(jax.random.fold_in(own_key, 6), dim), (shards_of,), jnp.float32, least / len(cuts), largest / len(cuts))
        loudness = loudness * jnp.repeat(jnp.exp(draws), extent[dim] // shards_of).reshape((-1,) + (1,) * (len(extent) - 1 - dim))
    return loudness


def bell_draw(rng, extent, spread, most, cuts=(), held_as=jnp.bfloat16):
    values = jax.random.normal(rng, extent, jnp.float32) * spread
    if len(cuts) > 0:
        values = levels(rng, extent, cuts, -0.22, 0.18) * values
    return jnp.clip(values, min=-most, max=most).astype(held_as)


def noise_with(rng, shape, deviation, limit, cuts, heavy, dtype=jnp.bfloat16):
    result = deviation * jax.random.normal(rng, shape, jnp.float32)
    if cuts:
        result = result * levels(rng, shape, cuts, -0.22, 0.18)
    return jnp.clip(strengthened(result, jax.random.fold_in(rng, 3), *heavy), -limit, limit).astype(dtype)


def setup_inputs(seed: int = 0) -> dict:
    arg_keys = jax.random.split(jax.random.key(seed), 7)
    out_grad = noise_with(arg_keys[0], (TOKENS, D), 1.0, 6.0, ((0, 16), (1, 16)), (0, 1, 16, 2.0))
    out_weight = bell_draw(arg_keys[1], (D, D), D ** -0.5, 0.0625, ((0, 16), (1, 16)))
    projections = bell_draw(arg_keys[2], (3, TOKENS, D), 1.0, 6.0, ((1, 16), (2, 16)))
    short_filters = bell_draw(arg_keys[3], (3, SHORT, D), 0.5, 3.0, ((2, 16),), jnp.float32)
    residues = bell_draw(arg_keys[4], (N_MODES, D), 0.01, 0.06, ((1, 16),), jnp.float32)
    decay_rates = jnp.clip(jnp.exp(math.log(0.05) - 6.931472 * jax.random.uniform(arg_keys[5], (N_MODES, D), jnp.float32) ** levels(arg_keys[5], (N_MODES, D), ((1, 16),), -0.2, 0.2)), 4.882812572759576e-05, 0.05)
    return dict(out_grad=out_grad, out_weight=out_weight, projections=projections, short_filters=short_filters, residues=residues, decay_rates=decay_rates)


def short_forward(padded, filters, length):
    total = filters[:, 0, None, :] * padded[:, SHORT - 1:SHORT - 1 + length, :]
    for offset in range(1, SHORT):
        total = total + filters[:, offset, None, :] * padded[:, SHORT - 1 - offset:SHORT - 1 - offset + length, :]
    return total


def channel_block(pieces):
    raw, filters, rates_block, residue_block, grad_y = pieces
    length = raw.shape[1]
    padded = jnp.pad(raw.astype(jnp.float32), ((0, 0), (SHORT - 1, 0), (0, 0)))
    branches = short_forward(padded, filters, length)
    q_branch, k_branch, v_branch = branches[0], branches[1], branches[2]
    product_kv = k_branch * v_branch
    decay = jnp.exp(-rates_block)

    def forward_step(state, value):
        state = decay * state + value[None, :]
        return state, state

    start_state = jnp.zeros(decay.shape, jnp.float32)
    _, states = lax.scan(forward_step, start_state, product_kv)
    long_out = jnp.sum(residue_block[None] * states, axis=1)
    y_rounded = (q_branch * long_out).astype(jnp.bfloat16)
    grad_long = grad_y * q_branch
    grad_q = grad_y * long_out

    def adjoint_step(state, value):
        state = decay * state + residue_block * value[None, :]
        return state, state

    _, adjoint = lax.scan(adjoint_step, start_state, grad_long, reverse=True)
    grad_kv = jnp.sum(adjoint, axis=1)
    grad_res = jnp.sum(grad_long[:, None, :] * states, axis=0)
    previous = jnp.concatenate([start_state[None], states[:-1]], axis=0)
    grad_rate = -decay * jnp.sum(adjoint * previous, axis=0)
    grad_branches = jnp.stack([grad_q, grad_kv * v_branch, grad_kv * k_branch])
    padded_back = jnp.pad(grad_branches, ((0, 0), (0, SHORT - 1), (0, 0)))
    grad_raw = filters[:, 0, None, :] * padded_back[:, 0:length, :]
    filter_terms = [jnp.sum(grad_branches * padded[:, SHORT - 1:SHORT - 1 + length, :], axis=1)]
    for offset in range(1, SHORT):
        grad_raw = grad_raw + filters[:, offset, None, :] * padded_back[:, offset:offset + length, :]
        filter_terms.append(jnp.sum(grad_branches * padded[:, SHORT - 1 - offset:SHORT - 1 - offset + length, :], axis=1))
    grad_filters = jnp.stack(filter_terms, axis=1)
    return grad_raw.astype(jnp.bfloat16), grad_filters, grad_res, grad_rate, y_rounded


def reference(out_grad, out_weight, projections, short_filters, residues, decay_rates):
    grad_y = jnp.dot(out_grad, out_weight, preferred_element_type=jnp.float32)
    width = math.gcd(D, 512)
    blocks = D // width

    def split(array):
        shaped = array.reshape(array.shape[:-1] + (blocks, width))
        return jnp.moveaxis(shaped, -2, 0)

    def join(array):
        moved = jnp.moveaxis(array, 0, -2)
        return moved.reshape(moved.shape[:-2] + (D,))

    pieces = (split(projections), split(short_filters), split(decay_rates), split(residues), split(grad_y))
    grad_raw, grad_filters, grad_res, grad_rate, y_rounded = lax.map(channel_block, pieces)
    grad_weight = lax.dot_general(out_grad, join(y_rounded), (((0,), (0,)), ((), ())), preferred_element_type=jnp.float32)
    return grad_weight.astype(jnp.bfloat16), join(grad_raw), join(grad_filters), join(grad_res), join(grad_rate)
```

```python
import jax
import jax.numpy as jnp
from jax import lax
from jax.experimental import pallas as pl
from jax.experimental.pallas import tpu as pltpu
from jax.sharding import Mesh
from jax.sharding import PartitionSpec as P

F32 = jnp.float32
BF16 = jnp.bfloat16
CTX = ("z", "xh")
FSDP = ("xl", "y", "core")
SUB = 32
NM = 16
STEPS = 32
NK = 16
ROWS = STEPS * NK
VMEM = pl.BlockSpec(memory_space=pltpu.VMEM)
RES, RATE, TAP = 0, 16, 32
PARAMS = pltpu.CompilerParams(vmem_limit_bytes=48 * 2**20)


def lane_group(shape):
    return lax.broadcasted_iota(jnp.int32, shape, len(shape) - 1) // SUB


def swap4(parts):
    group = lane_group(parts[0].shape)
    outs = []
    for r in range(4):
        total = None
        for q in range(4):
            turn = (SUB * (q - r)) % 128
            moved = parts[q] if turn == 0 else pltpu.roll(parts[q], turn, 1)
            total = moved if total is None else jnp.where(group == q, moved, total)
        outs.append(total)
    return outs


def shift_blocks(values, blocks, reverse=False):
    rows = values.shape[0]
    row = lax.broadcasted_iota(jnp.int32, values.shape, 0) % NK
    group = lane_group(values.shape)
    if blocks >= 4:
        by = blocks // 4
        if reverse:
            return jnp.where(row < NK - by, pltpu.roll(values, rows - by, 0), 0.0)
        return jnp.where(row >= by, pltpu.roll(values, by, 0), 0.0)
    if reverse:
        turned = pltpu.roll(values, 128 - SUB * blocks, 1)
        over = jnp.where(row < NK - 1, pltpu.roll(turned, rows - 1, 0), 0.0)
        return jnp.where(group >= 4 - blocks, over, turned)
    turned = pltpu.roll(values, SUB * blocks, 1)
    over = jnp.where(row >= 1, pltpu.roll(turned, 1, 0), 0.0)
    return jnp.where(group < blocks, over, turned)


def pack_kernel(x_ref, o_ref):
    for p in range(3):
        for g in range(4):
            parts = [
                x_ref[p, q * STEPS : (q + 1) * STEPS, g * 128 : (g + 1) * 128].astype(F32)
                for q in range(4)
            ]
            for r, out in enumerate(swap4(parts)):
                o_ref[4 * g + r, p * STEPS : (p + 1) * STEPS, :] = out.astype(BF16)


def prepare(x_ref, prm_ref, wide, x_ext, branch):
    wide[...] = x_ref[...].reshape(NK * 96, 128).astype(F32)
    for p in range(3):
        for t in range(STEPS):
            x_ext[p, (t + 2) * NK : (t + 3) * NK, :] = wide[pl.ds(p * STEPS + t, NK, stride=96), :]
        for back in range(2):
            x_ext[p, back * NK : (back + 1) * NK, :] = shift_blocks(
                x_ext[p, (STEPS + back) * NK : (STEPS + back + 1) * NK, :], 1
            )
        total = None
        for j in range(3):
            tap = prm_ref[TAP + 3 * p + j : TAP + 3 * p + j + 1, :]
            term = tap * x_ext[p, (2 - j) * NK : (2 - j) * NK + ROWS, :]
            total = term if total is None else total + term
        branch[p] = total


def spread(prm_ref, first, out):
    for n in range(NM):
        out[n * NK : (n + 1) * NK, :] = jnp.broadcast_to(
            prm_ref[first + n : first + n + 1, :], (NK, 128)
        )


def ends(source, decay8, out, reverse):
    for v in range(2):

        def step(i, state):
            t = STEPS - 1 - i if reverse else i
            value = source[pl.ds(pl.multiple_of(t * NK + v * 8, 8), 8), :]
            return tuple(decay8[n] * state[n] + value for n in range(NM))

        state = lax.fori_loop(
            0, STEPS, step, tuple(jnp.zeros((8, 128), F32) for _ in range(NM)), unroll=4
        )
        for n in range(NM):
            out[n * NK + v * 8 : n * NK + v * 8 + 8, :] = state[n]


def entering(ends_ref, rates, reverse):
    total = ends_ref[...]
    for log in range(6):
        blocks = 2**log
        power = jnp.exp(rates[...] * (-float(STEPS * blocks)))
        total = total + power * shift_blocks(total, blocks, reverse)
    return shift_blocks(total, 1, reverse)


def decays(prm_ref):
    return [
        jnp.exp(-jnp.broadcast_to(prm_ref[RATE + n : RATE + n + 1, :], (8, 128)))
        for n in range(NM)
    ]


def weights(prm_ref):
    return [jnp.broadcast_to(prm_ref[RES + n : RES + n + 1, :], (8, 128)) for n in range(NM)]


def forward_kernel(h_ref, x_ref, prm_ref, keep_ref, send_ref, in_ref, wide, x_ext, branch, kv, rates, tails, y):
    prepare(x_ref, prm_ref, wide, x_ext, branch)
    kv[...] = branch[1] * branch[2]
    spread(prm_ref, RATE, rates)
    decay8 = decays(prm_ref)
    ends(kv, decay8, tails, False)
    in_ref[...] = entering(tails, rates, False)
    weight8 = weights(prm_ref)
    for v in range(2):

        def step(t, state):
            at = pl.ds(pl.multiple_of(t * NK + v * 8, 8), 8)
            value = kv[at, :]
            state = tuple(decay8[n] * state[n] + value for n in range(NM))
            terms = [weight8[n] * state[n] for n in range(NM)]
            while len(terms) > 1:
                terms = [a + b for a, b in zip(terms[::2], terms[1::2])]
            y[at, :] = branch[0, at, :] * terms[0]
            return state

        lax.fori_loop(
            0,
            STEPS,
            step,
            tuple(in_ref[n * NK + v * 8 : n * NK + v * 8 + 8, :] for n in range(NM)),
            unroll=2,
        )
    h = h_ref[0]
    for k in range(8):
        keep_ref[k] = y[pl.ds(2 * k + h, STEPS, stride=NK), :].astype(BF16)
        send_ref[k] = y[pl.ds(2 * k + 1 - h, STEPS, stride=NK), :].astype(BF16)


def partial_kernel(at_ref, og_ref, own_ref, other_ref, o_ref):
    h = at_ref[1]
    total = jnp.dot(og_ref[0, h], own_ref[...], preferred_element_type=F32)
    total += jnp.dot(og_ref[0, 1 - h], other_ref[...], preferred_element_type=F32)
    for g in range(4):
        parts = [total[q * STEPS : (q + 1) * STEPS, g * 128 : (g + 1) * 128] for q in range(4)]
        for r, out in enumerate(swap4(parts)):
            o_ref[4 * g + r, 0] = out.astype(BF16)


def backward_kernel(x_ref, prm_ref, in_ref, gy_ref, o_ref, wide, x_ext, branch, kv, rates, tails, gy, gl, long_out, states, gkv, grads, raw, small, packed):
    prepare(x_ref, prm_ref, wide, x_ext, branch)
    kv[...] = branch[1] * branch[2]
    spread(prm_ref, RATE, rates)
    decay8 = decays(prm_ref)
    weight8 = weights(prm_ref)
    for n in range(NM):
        states[n, 0:NK, :] = in_ref[n * NK : (n + 1) * NK, :]
    for v in range(2):

        def forward(t, state):
            at = pl.ds(pl.multiple_of(t * NK + v * 8, 8), 8)
            value = kv[at, :]
            state = tuple(decay8[n] * state[n] + value for n in range(NM))
            later = pl.ds(pl.multiple_of((t + 1) * NK + v * 8, 8), 8)
            for n in range(NM):
                states[n, later, :] = state[n]
            terms = [weight8[n] * state[n] for n in range(NM)]
            while len(terms) > 1:
                terms = [a + b for a, b in zip(terms[::2], terms[1::2])]
            long_out[at, :] = terms[0]
            return state

        lax.fori_loop(
            0,
            STEPS,
            forward,
            tuple(in_ref[n * NK + v * 8 : n * NK + v * 8 + 8, :] for n in range(NM)),
            unroll=2,
        )
    for k in range(NK):
        total = gy_ref[0, k % 2, k // 2].astype(F32)
        for z in range(1, 8):
            total = total + gy_ref[z, k % 2, k // 2].astype(F32)
        wide[k * STEPS : (k + 1) * STEPS, :] = total
    for t in range(STEPS):
        gy[t * NK : (t + 1) * NK, :] = wide[pl.ds(t, NK, stride=STEPS), :]
    gl[...] = gy[...] * branch[0]
    grads[0, 0:ROWS, :] = gy[...] * long_out[...]
    ends(gl, decay8, tails, True)
    tails[...] = entering(tails, rates, True)
    zero = jnp.zeros((8, 128), F32)
    for half in range(2):
        modes = range(half * 8, half * 8 + 8)
        decay = [jnp.exp(-jnp.broadcast_to(prm_ref[RATE + n : RATE + n + 1, :], (8, 128))) for n in modes]
        weight = [jnp.broadcast_to(prm_ref[RES + n : RES + n + 1, :], (8, 128)) for n in modes]
        for v in range(2):

            def backward(i, carry):
                adjoint, by_res, by_rate = carry
                t = STEPS - 1 - i
                at = pl.ds(pl.multiple_of(t * NK + v * 8, 8), 8)
                later = pl.ds(pl.multiple_of((t + 1) * NK + v * 8, 8), 8)
                value = gl[at, :]
                adjoint = tuple(decay[m] * adjoint[m] + value for m in range(8))
                by_res = tuple(by_res[m] + value * states[n, later, :] for m, n in enumerate(modes))
                by_rate = tuple(
                    by_rate[m] + adjoint[m] * states[n, at, :] for m, n in enumerate(modes)
                )
                terms = [weight[m] * adjoint[m] for m in range(8)]
                while len(terms) > 1:
                    terms = [a + b for a, b in zip(terms[::2], terms[1::2])]
                if half == 0:
                    gkv[at, :] = terms[0]
                else:
                    gkv[at, :] = gkv[at, :] + terms[0]
                return adjoint, by_res, by_rate

            zeros = tuple(zero for _ in range(8))
            first = tuple(tails[n * NK + v * 8 : n * NK + v * 8 + 8, :] for n in modes)
            _, by_res, by_rate = lax.fori_loop(0, STEPS, backward, (first, zeros, zeros), unroll=2)
            for m, n in enumerate(modes):
                rate_part = by_rate[m] * (-decay[m] * weight[m])
                to_res = pl.ds((RES + n) * 8, 8)
                to_rate = pl.ds((RATE + n) * 8, 8)
                if v == 0:
                    small[to_res, :] = by_res[m]
                    small[to_rate, :] = rate_part
                else:
                    small[to_res, :] = small[to_res, :] + by_res[m]
                    small[to_rate, :] = small[to_rate, :] + rate_part
    grads[1, 0:ROWS, :] = gkv[...] * branch[2]
    grads[2, 0:ROWS, :] = gkv[...] * branch[1]
    for p in range(3):
        for ahead in range(2):
            grads[p, ROWS + ahead * NK : ROWS + (ahead + 1) * NK, :] = shift_blocks(
                grads[p, ahead * NK : (ahead + 1) * NK, :], 1, True
            )
        total = None
        for j in range(3):
            tap = prm_ref[TAP + 3 * p + j : TAP + 3 * p + j + 1, :]
            term = tap * grads[p, j * NK : j * NK + ROWS, :]
            total = term if total is None else total + term
            product = grads[p, 0:ROWS, :] * x_ext[p, (2 - j) * NK : (2 - j) * NK + ROWS, :]
            small[pl.ds((TAP + 3 * p + j) * 8, 8), :] = jnp.sum(
                product.reshape(ROWS // 8, 8, 128), axis=0
            )
        raw[p * ROWS : (p + 1) * ROWS, :] = total
    small[pl.ds((TAP + 9) * 8, 56), :] = jnp.zeros((56, 128), F32)
    total = small[pl.ds(0, 48, stride=8), :]
    for s in range(1, 8):
        total = total + small[pl.ds(s, 48, stride=8), :]
    total = total + pltpu.roll(total, 64, 1)
    total = total + pltpu.roll(total, 32, 1)
    high = total.astype(BF16).astype(F32)
    low = total - high
    group = lane_group((24, 128))
    packed[0:24, :] = jnp.where(
        group == 0,
        high[0:24],
        jnp.where(group == 1, low[0:24], jnp.where(group == 2, high[24:48], low[24:48])),
    )
    packed[24:32, :] = jnp.zeros((8, 128), F32)
    for k in range(NK):
        for p in range(3):
            o_ref[k, p * STEPS : (p + 1) * STEPS, :] = raw[
                pl.ds(p * ROWS + k, STEPS, stride=NK), :
            ].astype(BF16)
        o_ref[k, 96:128, :] = packed[...].astype(BF16)


def unpack_kernel(x_ref, gp_ref, short_ref, res_ref, rate_ref, small):
    group = lane_group((32, 128))
    for g in range(4):
        columns = slice(g * 128, (g + 1) * 128)
        for p in range(3):
            parts = [x_ref[4 * g + r, p * STEPS : (p + 1) * STEPS, :].astype(F32) for r in range(4)]
            for q, out in enumerate(swap4(parts)):
                gp_ref[p, q * STEPS : (q + 1) * STEPS, columns] = out.astype(BF16)
        first = second = jnp.zeros((32, 128), F32)
        for r in range(4):
            pair = x_ref[4 * g + r, 96:128, :].astype(F32)
            pair = pair + pltpu.roll(pair, 96, 1)
            one = pair if r == 0 else pltpu.roll(pair, SUB * r, 1)
            two = pair if r == 2 else pltpu.roll(pair, (SUB * (r - 2)) % 128, 1)
            first = jnp.where(group == r, one, first)
            second = jnp.where(group == r, two, second)
        small[0:24, columns] = first[0:24]
        small[24:48, columns] = second[0:24]
    res_ref[...] = small[RES : RES + NM, :]
    rate_ref[...] = small[RATE : RATE + NM, :]
    for p in range(3):
        short_ref[p] = small[TAP + 3 * p : TAP + 3 * p + 3, :]


def weight_kernel(at_ref, og_ref, y_ref, own_ref, send_ref, other, y):
    h = at_ref[1]
    step = pl.program_id(0)
    for g in range(4):
        parts = [y_ref[2 * g + r // 2, jnp.bitwise_xor(r % 2, h), 0].astype(F32) for r in range(4)]
        for q, out in enumerate(swap4(parts)):
            y[q * STEPS : (q + 1) * STEPS, g * 128 : (g + 1) * 128] = out.astype(BF16)
    over_rows = (((0,), (0,)), ((), ()))
    mine = lax.dot_general(og_ref[0, h], y[...], over_rows, preferred_element_type=F32)
    theirs = lax.dot_general(og_ref[0, 1 - h], y[...], over_rows, preferred_element_type=F32)

    @pl.when(step == 0)
    def _():
        own_ref[...] = mine
        other[...] = theirs

    @pl.when(step > 0)
    def _():
        own_ref[...] += mine
        other[...] += theirs

    @pl.when(step == pl.num_programs(0) - 1)
    def _():
        send_ref[...] = other[...].astype(BF16)


def shape(dims, dtype=F32):
    return jax.ShapeDtypeStruct(dims, dtype)


def scratch(*dims):
    return pltpu.VMEM(dims, F32)


SCANS = [
    scratch(NK * 96, 128),
    scratch(3, ROWS + 2 * NK, 128),
    scratch(3, ROWS, 128),
    scratch(ROWS, 128),
    scratch(NM * NK, 128),
    scratch(NM * NK, 128),
]
SWAP = [(0, 1), (1, 0)]


def on_device(out_grad, out_weight, projections, short_filters, residues, decay_rates):
    z, h = lax.axis_index("z"), lax.axis_index("xh")
    here = jnp.stack([z, h]).astype(jnp.int32)

    planes, spots = [], []
    for zz in range(8):
        for xl in range(2):
            for yy in range(4):
                to = 4 * xl + yy
                spot = (to - zz) % 8
                at = zz * 8 + xl * 4 + yy
                planes.append((at, zz * 8 + spot))
                spots.append((zz * 8 + spot, to * 8 + spot))
    moved = lax.ppermute(out_grad, ("z", "xl", "y"), planes)
    moved = lax.ppermute(moved, ("z", "xl", "y"), spots)
    other_weight = lax.ppermute(out_weight, "xh", SWAP)
    og = lax.all_gather(moved, FSDP, axis=0).reshape(8, 2, 128, 512)

    chunks = pl.pallas_call(pack_kernel, out_shape=shape((NK, 96, 128), BF16), in_specs=[VMEM], out_specs=VMEM)(projections)
    x = lax.all_to_all(chunks, CTX, 0, 0)
    prm = jnp.concatenate([residues, decay_rates, short_filters.reshape(9, 512)], axis=0)
    prm = lax.dynamic_slice(prm, (0, (2 * z + h) * SUB), (41, SUB))
    prm = jnp.pad(jnp.tile(prm, (1, 4)), ((0, 7), (0, 0)))

    keep, send, state_in = pl.pallas_call(
        forward_kernel,
        out_shape=(shape((8, STEPS, 128), BF16), shape((8, STEPS, 128), BF16), shape((NM * NK, 128))),
        in_specs=[pl.BlockSpec(memory_space=pltpu.SMEM), VMEM, VMEM],
        out_specs=(VMEM, VMEM, VMEM),
        scratch_shapes=SCANS + [scratch(ROWS, 128)],
        compiler_params=PARAMS,
    )(here[1:], x, prm)
    y = lax.all_gather(jnp.stack([keep, lax.ppermute(send, "xh", SWAP)]), "z", axis=0)

    parts = pl.pallas_call(
        partial_kernel,
        out_shape=shape((NK, 8, STEPS, 128), BF16),
        grid_spec=pltpu.PrefetchScalarGridSpec(
            num_scalar_prefetch=1,
            grid=(8,),
            in_specs=[
                pl.BlockSpec((1, 2, 128, 512), lambda p, at: (p, 0, 0, 0)),
                pl.BlockSpec((512, 512), lambda p, at: (0, 0)),
                pl.BlockSpec((512, 512), lambda p, at: (0, 0)),
            ],
            out_specs=pl.BlockSpec((NK, 1, STEPS, 128), lambda p, at: (0, (at[0] - p + 8) % 8, 0, 0)),
        ),
        compiler_params=PARAMS,
    )(here, og, out_weight, other_weight)
    grad_y = lax.all_to_all(parts, CTX, 0, 0).reshape(8, 2, 8, STEPS, 128)

    out = pl.pallas_call(
        backward_kernel,
        out_shape=shape((NK, 128, 128), BF16),
        in_specs=[VMEM] * 4,
        out_specs=VMEM,
        scratch_shapes=SCANS
        + [scratch(ROWS, 128)] * 3
        + [scratch(NM, ROWS + NK, 128), scratch(ROWS, 128), scratch(3, ROWS + 2 * NK, 128)]
        + [scratch(3 * ROWS, 128), scratch(48 * 8, 128), scratch(32, 128)],
        compiler_params=PARAMS,
    )(x, prm, state_in, grad_y)
    back = lax.all_to_all(out, CTX, 0, 0)
    grad_projections, grad_short, grad_res, grad_rate = pl.pallas_call(
        unpack_kernel,
        out_shape=(shape((3, 128, 512), BF16), shape((3, 3, 512)), shape((NM, 512)), shape((NM, 512))),
        in_specs=[VMEM],
        out_specs=(VMEM,) * 4,
        scratch_shapes=[scratch(48, 512)],
    )(back)

    own, send = pl.pallas_call(
        weight_kernel,
        out_shape=(shape((512, 512)), shape((512, 512), BF16)),
        grid_spec=pltpu.PrefetchScalarGridSpec(
            num_scalar_prefetch=1,
            grid=(8,),
            in_specs=[
                pl.BlockSpec((1, 2, 128, 512), lambda p, at: (p, 0, 0, 0)),
                pl.BlockSpec((8, 2, 1, STEPS, 128), lambda p, at: (0, 0, (at[0] - p + 8) % 8, 0, 0)),
            ],
            out_specs=[pl.BlockSpec((512, 512), lambda p, at: (0, 0))] * 2,
            scratch_shapes=[scratch(512, 512), pltpu.VMEM((128, 512), BF16)],
        ),
        compiler_params=PARAMS,
    )(here, og, y)
    grad_weight = (own + lax.ppermute(send, "xh", SWAP).astype(F32)).astype(BF16)
    return grad_weight, grad_projections, grad_short, grad_res, grad_rate


def solution(mesh):
    fine = Mesh(mesh.devices.reshape(8, 2, 2, 4, 2), CTX + FSDP)
    placed = (
        P(CTX, FSDP),
        P(CTX, FSDP),
        P(None, CTX, FSDP),
        P(None, None, FSDP),
        P(None, FSDP),
        P(None, FSDP),
    )
    return jax.shard_map(
        on_device,
        mesh=fine,
        in_specs=placed,
        out_specs=(
            P(CTX, FSDP),
            P(None, CTX, FSDP),
            P(None, None, FSDP),
            P(None, FSDP),
            P(None, FSDP),
        ),
        check_vma=False,
    )
```

```python
import jax
import jax.numpy as jnp
from jax import lax
from jax.experimental import pallas as pl
from jax.experimental.pallas import tpu as pltpu
from jax.sharding import Mesh
from jax.sharding import PartitionSpec as P


F32 = jnp.float32
BF16 = jnp.bfloat16
CTX = ("z", "xh")
FSDP = ("xl", "y", "core")
SUB = 32
NM = 16
STEPS = 32
NK = 16
ROWS = STEPS * NK
VMEM = pl.BlockSpec(memory_space=pltpu.VMEM)
RES, RATE, TAP = 0, 16, 32
PARAMS = pltpu.CompilerParams(vmem_limit_bytes=48 * 2**20)


def lane_group(shape):
    return lax.broadcasted_iota(jnp.int32, shape, len(shape) - 1) // SUB


def swap4(parts):
    group = lane_group(parts[0].shape)
    outs = []
    for r in range(4):
        total = None
        for q in range(4):
            turn = (SUB * (q - r)) % 128
            moved = parts[q] if turn == 0 else pltpu.roll(parts[q], turn, 1)
            total = moved if total is None else jnp.where(group == q, moved, total)
        outs.append(total)
    return outs


def shift_blocks(values, blocks, reverse=False):
    rows = values.shape[0]
    row = lax.broadcasted_iota(jnp.int32, values.shape, 0) % NK
    group = lane_group(values.shape)
    if blocks >= 4:
        by = blocks // 4
        if reverse:
            return jnp.where(row < NK - by, pltpu.roll(values, rows - by, 0), 0.0)
        return jnp.where(row >= by, pltpu.roll(values, by, 0), 0.0)
    if reverse:
        turned = pltpu.roll(values, 128 - SUB * blocks, 1)
        over = jnp.where(row < NK - 1, pltpu.roll(turned, rows - 1, 0), 0.0)
        return jnp.where(group >= 4 - blocks, over, turned)
    turned = pltpu.roll(values, SUB * blocks, 1)
    over = jnp.where(row >= 1, pltpu.roll(turned, 1, 0), 0.0)
    return jnp.where(group < blocks, over, turned)


def pack_kernel(at_ref, x_ref, res_ref, rate_ref, tap_ref, o_ref, prm_ref):
    for p in range(3):
        for g in range(4):
            parts = [
                x_ref[p, q * STEPS : (q + 1) * STEPS, g * 128 : (g + 1) * 128].astype(F32)
                for q in range(4)
            ]
            for r, out in enumerate(swap4(parts)):
                o_ref[4 * g + r, p * STEPS : (p + 1) * STEPS, :] = out.astype(BF16)
    m = at_ref[0]
    columns = pl.ds(pl.multiple_of(m // 4 * 128, 128), 128)

    def own(values):
        values = pltpu.roll(values, (4 - m % 4) % 4 * SUB, 1)
        values = jnp.where(lane_group(values.shape) == 0, values, 0.0)
        values = values + pltpu.roll(values, 64, 1)
        return values + pltpu.roll(values, 32, 1)

    prm_ref[RES : RES + NM, :] = own(res_ref[:, columns])
    prm_ref[RATE : RATE + NM, :] = own(rate_ref[:, columns])
    for p in range(3):
        prm_ref[TAP + 8 * p : TAP + 8 * p + 3, :] = own(tap_ref[p, :, columns])


def prepare(x_ref, prm_ref, wide, x_ext, branch):
    wide[...] = x_ref[...].reshape(NK * 96, 128).astype(F32)
    for p in range(3):
        for t in range(STEPS):
            x_ext[p, (t + 2) * NK : (t + 3) * NK, :] = wide[pl.ds(p * STEPS + t, NK, stride=96), :]
        for back in range(2):
            x_ext[p, back * NK : (back + 1) * NK, :] = shift_blocks(
                x_ext[p, (STEPS + back) * NK : (STEPS + back + 1) * NK, :], 1
            )
        total = None
        for j in range(3):
            tap = prm_ref[TAP + 8 * p + j : TAP + 8 * p + j + 1, :]
            term = tap * x_ext[p, (2 - j) * NK : (2 - j) * NK + ROWS, :]
            total = term if total is None else total + term
        branch[p] = total


def spread(prm_ref, first, out):
    for n in range(NM):
        out[n * NK : (n + 1) * NK, :] = jnp.broadcast_to(
            prm_ref[first + n : first + n + 1, :], (NK, 128)
        )


def ends(source, decay8, out, reverse):
    for v in range(2):

        def step(i, state):
            t = STEPS - 1 - i if reverse else i
            value = source[pl.ds(pl.multiple_of(t * NK + v * 8, 8), 8), :]
            return tuple(decay8[n] * state[n] + value for n in range(NM))

        state = lax.fori_loop(
            0, STEPS, step, tuple(jnp.zeros((8, 128), F32) for _ in range(NM)), unroll=4
        )
        for n in range(NM):
            out[n * NK + v * 8 : n * NK + v * 8 + 8, :] = state[n]


def entering(ends_ref, rates, reverse):
    total = ends_ref[...]
    for log in range(6):
        blocks = 2**log
        power = jnp.exp(rates[...] * (-float(STEPS * blocks)))
        total = total + power * shift_blocks(total, blocks, reverse)
    return shift_blocks(total, 1, reverse)


def decays(prm_ref):
    return [
        jnp.exp(-jnp.broadcast_to(prm_ref[RATE + n : RATE + n + 1, :], (8, 128)))
        for n in range(NM)
    ]


def weights(prm_ref):
    return [jnp.broadcast_to(prm_ref[RES + n : RES + n + 1, :], (8, 128)) for n in range(NM)]


def forward_kernel(at_ref, x_ref, prm_ref, keep_ref, send_ref, in_ref, wide, x_ext, branch, kv, rates, tails, y):
    prepare(x_ref, prm_ref, wide, x_ext, branch)
    kv[...] = branch[1] * branch[2]
    spread(prm_ref, RATE, rates)
    decay8 = decays(prm_ref)
    ends(kv, decay8, tails, False)
    in_ref[...] = entering(tails, rates, False)
    weight8 = weights(prm_ref)
    for v in range(2):

        def step(t, state):
            at = pl.ds(pl.multiple_of(t * NK + v * 8, 8), 8)
            value = kv[at, :]
            state = tuple(decay8[n] * state[n] + value for n in range(NM))
            terms = [weight8[n] * state[n] for n in range(NM)]
            while len(terms) > 1:
                terms = [a + b for a, b in zip(terms[::2], terms[1::2])]
            y[at, :] = branch[0, at, :] * terms[0]
            return state

        lax.fori_loop(
            0,
            STEPS,
            step,
            tuple(in_ref[n * NK + v * 8 : n * NK + v * 8 + 8, :] for n in range(NM)),
            unroll=2,
        )
    h = at_ref[1]
    for k in range(8):
        keep_ref[k] = y[pl.ds(2 * k + h, STEPS, stride=NK), :].astype(BF16)
        send_ref[k] = y[pl.ds(2 * k + 1 - h, STEPS, stride=NK), :].astype(BF16)


BATCHES = ((0, 4, 1, 3), (5, 7, 2, 6))


def shard_of(z, spot, away):
    return (z - jnp.bitwise_xor(spot, away) + 8) % 8


def partial_kernel(at_ref, mine_ref, theirs_ref, w0_ref, w1_ref, after_ref, o_ref, rows_ref):
    own_first = at_ref[1] == at_ref[2]
    for i in range(4):
        mine, theirs = mine_ref[i], theirs_ref[i]
        rows_ref[0, i * 128 : (i + 1) * 128, :] = jnp.where(own_first, mine, theirs)
        rows_ref[1, i * 128 : (i + 1) * 128, :] = jnp.where(own_first, theirs, mine)
    for i in range(4):
        total = jnp.dot(
            rows_ref[0, i * 128 : (i + 1) * 128, :], w0_ref[...], preferred_element_type=F32
        ) + jnp.dot(
            rows_ref[1, i * 128 : (i + 1) * 128, :], w1_ref[...], preferred_element_type=F32
        )
        for g in range(4):
            parts = [total[q * STEPS : (q + 1) * STEPS, g * 128 : (g + 1) * 128] for q in range(4)]
            for r, out in enumerate(swap4(parts)):
                o_ref[4 * g + r, i] = out.astype(BF16)


def backward_kernel(at_ref, x_ref, prm_ref, in_ref, gy1_ref, gy2_ref, o_ref, wide, x_ext, branch, kv, rates, tails, gy, gl, long_out, states, gkv, grads, raw, small, packed):
    prepare(x_ref, prm_ref, wide, x_ext, branch)
    kv[...] = branch[1] * branch[2]
    spread(prm_ref, RATE, rates)
    decay8 = decays(prm_ref)
    weight8 = weights(prm_ref)
    for n in range(NM):
        states[n, 0:NK, :] = in_ref[n * NK : (n + 1) * NK, :]
    for v in range(2):

        def forward(t, state):
            at = pl.ds(pl.multiple_of(t * NK + v * 8, 8), 8)
            value = kv[at, :]
            state = tuple(decay8[n] * state[n] + value for n in range(NM))
            later = pl.ds(pl.multiple_of((t + 1) * NK + v * 8, 8), 8)
            for n in range(NM):
                states[n, later, :] = state[n]
            terms = [weight8[n] * state[n] for n in range(NM)]
            while len(terms) > 1:
                terms = [a + b for a, b in zip(terms[::2], terms[1::2])]
            long_out[at, :] = terms[0]
            return state

        lax.fori_loop(
            0,
            STEPS,
            forward,
            tuple(in_ref[n * NK + v * 8 : n * NK + v * 8 + 8, :] for n in range(NM)),
            unroll=2,
        )
    spot = at_ref[3]
    wide[0:ROWS, :] = jnp.zeros((ROWS, 128), F32)
    for batch, gy_ref in zip(BATCHES, (gy1_ref, gy2_ref)):
        for i, away in enumerate(batch):
            for source in range(NK):
                k = 2 * shard_of(source // 2, spot, away) + source % 2
                at = pl.ds(pl.multiple_of(k * STEPS, STEPS), STEPS)
                wide[at, :] = wide[at, :] + gy_ref[source, i].astype(F32)
    for t in range(STEPS):
        gy[t * NK : (t + 1) * NK, :] = wide[pl.ds(t, NK, stride=STEPS), :]
    gl[...] = gy[...] * branch[0]
    grads[0, 0:ROWS, :] = gy[...] * long_out[...]
    ends(gl, decay8, tails, True)
    tails[...] = entering(tails, rates, True)
    zero = jnp.zeros((8, 128), F32)
    for half in range(2):
        modes = range(half * 8, half * 8 + 8)
        decay = [jnp.exp(-jnp.broadcast_to(prm_ref[RATE + n : RATE + n + 1, :], (8, 128))) for n in modes]
        weight = [jnp.broadcast_to(prm_ref[RES + n : RES + n + 1, :], (8, 128)) for n in modes]
        for v in range(2):

            def backward(i, carry):
                adjoint, by_res, by_rate = carry
                t = STEPS - 1 - i
                at = pl.ds(pl.multiple_of(t * NK + v * 8, 8), 8)
                later = pl.ds(pl.multiple_of((t + 1) * NK + v * 8, 8), 8)
                value = gl[at, :]
                adjoint = tuple(decay[m] * adjoint[m] + value for m in range(8))
                by_res = tuple(by_res[m] + value * states[n, later, :] for m, n in enumerate(modes))
                by_rate = tuple(
                    by_rate[m] + adjoint[m] * states[n, at, :] for m, n in enumerate(modes)
                )
                terms = [weight[m] * adjoint[m] for m in range(8)]
                while len(terms) > 1:
                    terms = [a + b for a, b in zip(terms[::2], terms[1::2])]
                if half == 0:
                    gkv[at, :] = terms[0]
                else:
                    gkv[at, :] = gkv[at, :] + terms[0]
                return adjoint, by_res, by_rate

            zeros = tuple(zero for _ in range(8))
            first = tuple(tails[n * NK + v * 8 : n * NK + v * 8 + 8, :] for n in modes)
            _, by_res, by_rate = lax.fori_loop(0, STEPS, backward, (first, zeros, zeros), unroll=2)
            for m, n in enumerate(modes):
                rate_part = by_rate[m] * (-decay[m] * weight[m])
                to_res = pl.ds((RES + n) * 8, 8)
                to_rate = pl.ds((RATE + n) * 8, 8)
                if v == 0:
                    small[to_res, :] = by_res[m]
                    small[to_rate, :] = rate_part
                else:
                    small[to_res, :] = small[to_res, :] + by_res[m]
                    small[to_rate, :] = small[to_rate, :] + rate_part
    grads[1, 0:ROWS, :] = gkv[...] * branch[2]
    grads[2, 0:ROWS, :] = gkv[...] * branch[1]
    for p in range(3):
        for ahead in range(2):
            grads[p, ROWS + ahead * NK : ROWS + (ahead + 1) * NK, :] = shift_blocks(
                grads[p, ahead * NK : (ahead + 1) * NK, :], 1, True
            )
        total = None
        for j in range(3):
            tap = prm_ref[TAP + 8 * p + j : TAP + 8 * p + j + 1, :]
            term = tap * grads[p, j * NK : j * NK + ROWS, :]
            total = term if total is None else total + term
            product = grads[p, 0:ROWS, :] * x_ext[p, (2 - j) * NK : (2 - j) * NK + ROWS, :]
            small[pl.ds((TAP + 3 * p + j) * 8, 8), :] = jnp.sum(
                product.reshape(ROWS // 8, 8, 128), axis=0
            )
        raw[p * ROWS : (p + 1) * ROWS, :] = total
    small[pl.ds((TAP + 9) * 8, 56), :] = jnp.zeros((56, 128), F32)
    total = small[pl.ds(0, 48, stride=8), :]
    for s in range(1, 8):
        total = total + small[pl.ds(s, 48, stride=8), :]
    total = total + pltpu.roll(total, 64, 1)
    total = total + pltpu.roll(total, 32, 1)
    high = total.astype(BF16).astype(F32)
    low = total - high
    group = lane_group((24, 128))
    packed[0:24, :] = jnp.where(
        group == 0,
        high[0:24],
        jnp.where(group == 1, low[0:24], jnp.where(group == 2, high[24:48], low[24:48])),
    )
    packed[24:32, :] = jnp.zeros((8, 128), F32)
    for k in range(NK):
        for p in range(3):
            o_ref[k, p * STEPS : (p + 1) * STEPS, :] = raw[
                pl.ds(p * ROWS + k, STEPS, stride=NK), :
            ].astype(BF16)
        o_ref[k, 96:128, :] = packed[...].astype(BF16)


def unpack_kernel(x_ref, gp_ref, short_ref, res_ref, rate_ref, small):
    group = lane_group((32, 128))
    for g in range(4):
        columns = slice(g * 128, (g + 1) * 128)
        for p in range(3):
            parts = [x_ref[4 * g + r, p * STEPS : (p + 1) * STEPS, :].astype(F32) for r in range(4)]
            for q, out in enumerate(swap4(parts)):
                gp_ref[p, q * STEPS : (q + 1) * STEPS, columns] = out.astype(BF16)
        first = second = jnp.zeros((32, 128), F32)
        for r in range(4):
            pair = x_ref[4 * g + r, 96:128, :].astype(F32)
            pair = pair + pltpu.roll(pair, 96, 1)
            one = pair if r == 0 else pltpu.roll(pair, SUB * r, 1)
            two = pair if r == 2 else pltpu.roll(pair, (SUB * (r - 2)) % 128, 1)
            first = jnp.where(group == r, one, first)
            second = jnp.where(group == r, two, second)
        small[0:24, columns] = first[0:24]
        small[24:48, columns] = second[0:24]
    res_ref[...] = small[RES : RES + NM, :]
    rate_ref[...] = small[RATE : RATE + NM, :]
    for p in range(3):
        short_ref[p] = small[TAP + 3 * p : TAP + 3 * p + 3, :]


def weight_kernel(at_ref, rows1_ref, rows2_ref, y0, r1, r2, r3, r4, l3, l2, l1, own_ref, send_ref, y_all, y):
    z, h, spot = at_ref[0], at_ref[1], at_ref[3]
    for back, y_ref in enumerate((y0, r1, r2, r3, r4, l3, l2, l1)):
        y_all[(z - back + 8) % 8] = y_ref[...]
    for b, batch in enumerate(BATCHES):
        for i, away in enumerate(batch):
            k = shard_of(z, spot, away)
            for g in range(4):
                parts = [
                    y_all[2 * g + r // 2, jnp.bitwise_xor(r % 2, h), k].astype(F32)
                    for r in range(4)
                ]
                for q, out in enumerate(swap4(parts)):
                    first = b * 512 + i * 128 + q * STEPS
                    y[first : first + STEPS, g * 128 : (g + 1) * 128] = out.astype(BF16)
    over_rows = (((0,), (0,)), ((), ()))
    for x, out_ref in enumerate((own_ref, send_ref)):
        total = lax.dot_general(rows1_ref[x], y[0:512, :], over_rows, preferred_element_type=F32)
        total += lax.dot_general(
            rows2_ref[x], y[512:1024, :], over_rows, preferred_element_type=F32
        )
        out_ref[...] = total.astype(out_ref.dtype)


def shape(dims, dtype=F32):
    return jax.ShapeDtypeStruct(dims, dtype)


def scratch(*dims):
    return pltpu.VMEM(dims, F32)


SCANS = [
    scratch(NK * 96, 128),
    scratch(3, ROWS + 2 * NK, 128),
    scratch(3, ROWS, 128),
    scratch(ROWS, 128),
    scratch(NM * NK, 128),
    scratch(NM * NK, 128),
]


def call(kernel, **settings):
    def run(*args):
        return pl.pallas_call(kernel, **settings)(*args)

    return run


def compute(out_grad, out_weight, projections, short_filters, residues, decay_rates):
    z, h, xl, spot_y, core = (lax.axis_index(a) for a in CTX + FSDP)
    here = jnp.stack([z, h, core, 4 * xl + spot_y, 2 * z + h]).astype(jnp.int32)

    route = [
        (zz * 8 + at, at * 8 + (at - zz) % 8) for zz in range(8) for at in range(8)
    ]
    moved = lax.ppermute(out_grad, ("z", "xl", "y"), route)

    def flip(value, axis, by):
        return lax.ppermute(value, axis, [(i, i ^ by) for i in range(lax.axis_size(axis))])

    across = flip(moved, "xl", 1)
    near, wrap = flip(moved, "y", 1), flip(moved, "y", 3)
    near2, wrap2 = flip(across, "y", 1), flip(across, "y", 3)
    far, far2 = flip(wrap, "y", 1), flip(near2, "y", 3)
    mine1 = jnp.stack([moved, across, near, wrap])
    mine2 = jnp.stack([near2, wrap2, far, far2])
    theirs1, theirs2 = flip(mine1, "core", 1), flip(mine2, "core", 1)
    other_weight = flip(out_weight, "xh", 1)

    chunks, prm = call(
        pack_kernel,
        out_shape=(shape((NK, 96, 128), BF16), shape((56, 128))),
        in_specs=[pl.BlockSpec(memory_space=pltpu.SMEM)] + [VMEM] * 4,
        out_specs=(VMEM, VMEM),
    )(here[4:], projections, residues, decay_rates, short_filters)
    x = lax.all_to_all(chunks, CTX, 0, 0)

    smem = pl.BlockSpec(memory_space=pltpu.SMEM)
    keep, send, state_in = call(
        forward_kernel,
        out_shape=(shape((8, STEPS, 128), BF16), shape((8, STEPS, 128), BF16), shape((NM * NK, 128))),
        in_specs=[smem, VMEM, VMEM],
        out_specs=(VMEM,) * 3,
        scratch_shapes=SCANS + [scratch(ROWS, 128)],
        compiler_params=PARAMS,
    )(here, x, prm)

    def turn(value, by):
        return lax.ppermute(value, "z", [(i, (i + by) % 8) for i in range(8)])

    y0 = jnp.stack([keep, flip(send, "xh", 1)])
    r1, l1 = turn(y0, 1), turn(y0, -1)
    r2, l2 = turn(r1, 1), turn(l1, -1)
    r3, l3 = turn(r2, 1), turn(l2, -1)
    r4 = turn(r2, 2)

    grads, rows, after = [], [], state_in
    for mine, theirs in ((mine1, theirs1), (mine2, theirs2)):
        parts, blocks = call(
            partial_kernel,
            out_shape=(shape((NK, 4, STEPS, 128), BF16), shape((2, 512, 512), BF16)),
            in_specs=[smem] + [VMEM] * 4 + [pl.BlockSpec(memory_space=pl.ANY)],
            out_specs=(VMEM, VMEM),
            compiler_params=PARAMS,
        )(here, mine, theirs, out_weight, other_weight, after)
        grads.append(lax.all_to_all(parts, CTX, 0, 0))
        rows.append(blocks)

    out = call(
        backward_kernel,
        out_shape=shape((NK, 128, 128), BF16),
        in_specs=[smem] + [VMEM] * 5,
        out_specs=VMEM,
        scratch_shapes=SCANS
        + [scratch(ROWS, 128)] * 3
        + [scratch(NM, ROWS + NK, 128), scratch(ROWS, 128), scratch(3, ROWS + 2 * NK, 128)]
        + [scratch(3 * ROWS, 128), scratch(48 * 8, 128), scratch(32, 128)],
        compiler_params=PARAMS,
    )(here, x, prm, state_in, *grads)
    back = lax.all_to_all(out, CTX, 0, 0)
    grad_projections, grad_short, grad_res, grad_rate = call(
        unpack_kernel,
        out_shape=(shape((3, 128, 512), BF16), shape((3, 3, 512)), shape((NM, 512)), shape((NM, 512))),
        in_specs=[VMEM],
        out_specs=(VMEM,) * 4,
        scratch_shapes=[scratch(48, 512)],
    )(back)

    own, send = call(
        weight_kernel,
        out_shape=(shape((512, 512)), shape((512, 512), BF16)),
        in_specs=[smem] + [VMEM] * 10,
        out_specs=(VMEM, VMEM),
        scratch_shapes=[pltpu.VMEM((8, 2, 8, STEPS, 128), BF16), pltpu.VMEM((1024, 512), BF16)],
        compiler_params=PARAMS,
    )(here, *rows, y0, r1, r2, r3, r4, l3, l2, l1)
    grad_weight = (own + flip(send, "xh", 1).astype(F32)).astype(BF16)
    return grad_weight, grad_projections, grad_short, grad_res, grad_rate


def solution(mesh):
    fine = Mesh(mesh.devices.reshape(8, 2, 2, 4, 2), CTX + FSDP)
    placed = (
        P(CTX, FSDP),
        P(CTX, FSDP),
        P(None, CTX, FSDP),
        P(None, None, FSDP),
        P(None, FSDP),
        P(None, FSDP),
    )
    return jax.shard_map(
        compute,
        mesh=fine,
        in_specs=placed,
        out_specs=(
            P(CTX, FSDP),
            P(None, CTX, FSDP),
            P(None, None, FSDP),
            P(None, FSDP),
            P(None, FSDP),
        ),
        check_vma=False,
    )
```

```python
import jax
import jax.numpy as jnp
from jax import lax
from jax.experimental import pallas as pl
from jax.experimental.pallas import tpu as pltpu
from jax.sharding import Mesh
from jax.sharding import PartitionSpec as P


F32 = jnp.float32
BF16 = jnp.bfloat16
CTX = ("z", "xh")
FSDP = ("xl", "y", "core")
SUB = 32
NM = 16
STEPS = 32
NK = 16
ROWS = STEPS * NK
VMEM = pl.BlockSpec(memory_space=pltpu.VMEM)
RES, RATE, TAP = 0, 16, 32
PARAMS = pltpu.CompilerParams(vmem_limit_bytes=48 * 2**20)


def lane_group(shape):
    return lax.broadcasted_iota(jnp.int32, shape, len(shape) - 1) // SUB


def swap4(parts):
    group = lane_group(parts[0].shape)
    outs = []
    for r in range(4):
        total = None
        for q in range(4):
            turn = (SUB * (q - r)) % 128
            moved = parts[q] if turn == 0 else pltpu.roll(parts[q], turn, 1)
            total = moved if total is None else jnp.where(group == q, moved, total)
        outs.append(total)
    return outs


def shift_blocks(values, blocks, reverse=False):
    rows = values.shape[0]
    row = lax.broadcasted_iota(jnp.int32, values.shape, 0) % NK
    group = lane_group(values.shape)
    if blocks >= 4:
        by = blocks // 4
        if reverse:
            return jnp.where(row < NK - by, pltpu.roll(values, rows - by, 0), 0.0)
        return jnp.where(row >= by, pltpu.roll(values, by, 0), 0.0)
    if reverse:
        turned = pltpu.roll(values, 128 - SUB * blocks, 1)
        over = jnp.where(row < NK - 1, pltpu.roll(turned, rows - 1, 0), 0.0)
        return jnp.where(group >= 4 - blocks, over, turned)
    turned = pltpu.roll(values, SUB * blocks, 1)
    over = jnp.where(row >= 1, pltpu.roll(turned, 1, 0), 0.0)
    return jnp.where(group < blocks, over, turned)


def pack_kernel(at_ref, x_ref, res_ref, rate_ref, tap_ref, o_ref, prm_ref):
    for p in range(3):
        for g in range(4):
            parts = [
                x_ref[p, q * STEPS : (q + 1) * STEPS, g * 128 : (g + 1) * 128].astype(F32)
                for q in range(4)
            ]
            for r, out in enumerate(swap4(parts)):
                o_ref[4 * g + r, p * STEPS : (p + 1) * STEPS, :] = out.astype(BF16)
    m = at_ref[0]
    columns = pl.ds(pl.multiple_of(m // 4 * 128, 128), 128)

    def own(values):
        values = pltpu.roll(values, (4 - m % 4) % 4 * SUB, 1)
        values = jnp.where(lane_group(values.shape) == 0, values, 0.0)
        values = values + pltpu.roll(values, 64, 1)
        return values + pltpu.roll(values, 32, 1)

    prm_ref[RES : RES + NM, :] = own(res_ref[:, columns])
    prm_ref[RATE : RATE + NM, :] = own(rate_ref[:, columns])
    for p in range(3):
        prm_ref[TAP + 8 * p : TAP + 8 * p + 3, :] = own(tap_ref[p, :, columns])


def prepare(x_ref, prm_ref, wide, x_ext, branch):
    wide[...] = x_ref[...].reshape(NK * 96, 128).astype(F32)
    for p in range(3):
        for t in range(STEPS):
            x_ext[p, (t + 2) * NK : (t + 3) * NK, :] = wide[pl.ds(p * STEPS + t, NK, stride=96), :]
        for back in range(2):
            x_ext[p, back * NK : (back + 1) * NK, :] = shift_blocks(
                x_ext[p, (STEPS + back) * NK : (STEPS + back + 1) * NK, :], 1
            )
        total = None
        for j in range(3):
            tap = prm_ref[TAP + 8 * p + j : TAP + 8 * p + j + 1, :]
            term = tap * x_ext[p, (2 - j) * NK : (2 - j) * NK + ROWS, :]
            total = term if total is None else total + term
        branch[p] = total


def spread(prm_ref, first, out):
    for n in range(NM):
        out[n * NK : (n + 1) * NK, :] = jnp.broadcast_to(
            prm_ref[first + n : first + n + 1, :], (NK, 128)
        )


def ends(source, decay8, out, reverse):
    for v in range(2):

        def step(i, state):
            t = STEPS - 1 - i if reverse else i
            value = source[pl.ds(pl.multiple_of(t * NK + v * 8, 8), 8), :]
            return tuple(decay8[n] * state[n] + value for n in range(NM))

        state = lax.fori_loop(
            0, STEPS, step, tuple(jnp.zeros((8, 128), F32) for _ in range(NM)), unroll=4
        )
        for n in range(NM):
            out[n * NK + v * 8 : n * NK + v * 8 + 8, :] = state[n]


def entering(ends_ref, rates, reverse):
    total = ends_ref[...]
    for log in range(6):
        blocks = 2**log
        power = jnp.exp(rates[...] * (-float(STEPS * blocks)))
        total = total + power * shift_blocks(total, blocks, reverse)
    return shift_blocks(total, 1, reverse)


def decays(prm_ref):
    return [
        jnp.exp(-jnp.broadcast_to(prm_ref[RATE + n : RATE + n + 1, :], (8, 128)))
        for n in range(NM)
    ]


def weights(prm_ref):
    return [jnp.broadcast_to(prm_ref[RES + n : RES + n + 1, :], (8, 128)) for n in range(NM)]


def forward_kernel(at_ref, x_ref, prm_ref, keep_ref, send_ref, in_ref, wide, x_ext, branch, kv, rates, tails, y):
    prepare(x_ref, prm_ref, wide, x_ext, branch)
    kv[...] = branch[1] * branch[2]
    spread(prm_ref, RATE, rates)
    decay8 = decays(prm_ref)
    ends(kv, decay8, tails, False)
    in_ref[...] = entering(tails, rates, False)
    weight8 = weights(prm_ref)
    for v in range(2):

        def step(t, state):
            at = pl.ds(pl.multiple_of(t * NK + v * 8, 8), 8)
            value = kv[at, :]
            state = tuple(decay8[n] * state[n] + value for n in range(NM))
            terms = [weight8[n] * state[n] for n in range(NM)]
            while len(terms) > 1:
                terms = [a + b for a, b in zip(terms[::2], terms[1::2])]
            y[at, :] = branch[0, at, :] * terms[0]
            return state

        lax.fori_loop(
            0,
            STEPS,
            step,
            tuple(in_ref[n * NK + v * 8 : n * NK + v * 8 + 8, :] for n in range(NM)),
            unroll=2,
        )
    h = at_ref[1]
    for k in range(8):
        keep_ref[k] = y[pl.ds(2 * k + h, STEPS, stride=NK), :].astype(BF16)
        send_ref[k] = y[pl.ds(2 * k + 1 - h, STEPS, stride=NK), :].astype(BF16)


BATCHES = ((0, 4, 1, 3), (5, 7, 2, 6))


def shard_of(z, spot, away):
    return (z - jnp.bitwise_xor(spot, away) + 8) % 8


def partial_kernel(at_ref, mine_ref, theirs_ref, w0_ref, w1_ref, after_ref, o_ref, rows_ref):
    own_first = at_ref[1] == at_ref[2]
    for i in range(4):
        mine, theirs = mine_ref[i], theirs_ref[i]
        rows_ref[0, i * 128 : (i + 1) * 128, :] = jnp.where(own_first, mine, theirs)
        rows_ref[1, i * 128 : (i + 1) * 128, :] = jnp.where(own_first, theirs, mine)
    for i in range(4):
        total = jnp.dot(
            rows_ref[0, i * 128 : (i + 1) * 128, :], w0_ref[...], preferred_element_type=F32
        ) + jnp.dot(
            rows_ref[1, i * 128 : (i + 1) * 128, :], w1_ref[...], preferred_element_type=F32
        )
        for g in range(4):
            parts = [total[q * STEPS : (q + 1) * STEPS, g * 128 : (g + 1) * 128] for q in range(4)]
            for r, out in enumerate(swap4(parts)):
                o_ref[4 * g + r, i] = out.astype(BF16)


def backward_kernel(at_ref, x_ref, prm_ref, in_ref, gy1_ref, gy2_ref, o_ref, wide, x_ext, branch, kv, rates, tails, gy, gl, long_out, states, gkv, grads, raw, small, packed):
    prepare(x_ref, prm_ref, wide, x_ext, branch)
    kv[...] = branch[1] * branch[2]
    spread(prm_ref, RATE, rates)
    decay8 = decays(prm_ref)
    weight8 = weights(prm_ref)
    for n in range(NM):
        states[n, 0:NK, :] = in_ref[n * NK : (n + 1) * NK, :]
    for v in range(2):

        def forward(t, state):
            at = pl.ds(pl.multiple_of(t * NK + v * 8, 8), 8)
            value = kv[at, :]
            state = tuple(decay8[n] * state[n] + value for n in range(NM))
            later = pl.ds(pl.multiple_of((t + 1) * NK + v * 8, 8), 8)
            for n in range(NM):
                states[n, later, :] = state[n]
            terms = [weight8[n] * state[n] for n in range(NM)]
            while len(terms) > 1:
                terms = [a + b for a, b in zip(terms[::2], terms[1::2])]
            long_out[at, :] = terms[0]
            return state

        lax.fori_loop(
            0,
            STEPS,
            forward,
            tuple(in_ref[n * NK + v * 8 : n * NK + v * 8 + 8, :] for n in range(NM)),
            unroll=2,
        )
    spot = at_ref[3]
    wide[0:ROWS, :] = jnp.zeros((ROWS, 128), F32)
    for batch, gy_ref in zip(BATCHES, (gy1_ref, gy2_ref)):
        for i, away in enumerate(batch):
            for source in range(NK):
                k = 2 * shard_of(source // 2, spot, away) + source % 2
                at = pl.ds(pl.multiple_of(k * STEPS, STEPS), STEPS)
                wide[at, :] = wide[at, :] + gy_ref[source, i].astype(F32)
    for t in range(STEPS):
        gy[t * NK : (t + 1) * NK, :] = wide[pl.ds(t, NK, stride=STEPS), :]
    gl[...] = gy[...] * branch[0]
    grads[0, 0:ROWS, :] = gy[...] * long_out[...]
    ends(gl, decay8, tails, True)
    tails[...] = entering(tails, rates, True)
    zero = jnp.zeros((8, 128), F32)
    for half in range(2):
        modes = range(half * 8, half * 8 + 8)
        decay = [jnp.exp(-jnp.broadcast_to(prm_ref[RATE + n : RATE + n + 1, :], (8, 128))) for n in modes]
        weight = [jnp.broadcast_to(prm_ref[RES + n : RES + n + 1, :], (8, 128)) for n in modes]
        for v in range(2):

            def backward(i, carry):
                adjoint, by_res, by_rate = carry
                t = STEPS - 1 - i
                at = pl.ds(pl.multiple_of(t * NK + v * 8, 8), 8)
                later = pl.ds(pl.multiple_of((t + 1) * NK + v * 8, 8), 8)
                value = gl[at, :]
                adjoint = tuple(decay[m] * adjoint[m] + value for m in range(8))
                by_res = tuple(by_res[m] + value * states[n, later, :] for m, n in enumerate(modes))
                by_rate = tuple(
                    by_rate[m] + adjoint[m] * states[n, at, :] for m, n in enumerate(modes)
                )
                terms = [weight[m] * adjoint[m] for m in range(8)]
                while len(terms) > 1:
                    terms = [a + b for a, b in zip(terms[::2], terms[1::2])]
                if half == 0:
                    gkv[at, :] = terms[0]
                else:
                    gkv[at, :] = gkv[at, :] + terms[0]
                return adjoint, by_res, by_rate

            zeros = tuple(zero for _ in range(8))
            first = tuple(tails[n * NK + v * 8 : n * NK + v * 8 + 8, :] for n in modes)
            _, by_res, by_rate = lax.fori_loop(0, STEPS, backward, (first, zeros, zeros), unroll=2)
            for m, n in enumerate(modes):
                rate_part = by_rate[m] * (-decay[m] * weight[m])
                to_res = pl.ds((RES + n) * 8, 8)
                to_rate = pl.ds((RATE + n) * 8, 8)
                if v == 0:
                    small[to_res, :] = by_res[m]
                    small[to_rate, :] = rate_part
                else:
                    small[to_res, :] = small[to_res, :] + by_res[m]
                    small[to_rate, :] = small[to_rate, :] + rate_part
    grads[1, 0:ROWS, :] = gkv[...] * branch[2]
    grads[2, 0:ROWS, :] = gkv[...] * branch[1]
    for p in range(3):
        for ahead in range(2):
            grads[p, ROWS + ahead * NK : ROWS + (ahead + 1) * NK, :] = shift_blocks(
                grads[p, ahead * NK : (ahead + 1) * NK, :], 1, True
            )
        total = None
        for j in range(3):
            tap = prm_ref[TAP + 8 * p + j : TAP + 8 * p + j + 1, :]
            term = tap * grads[p, j * NK : j * NK + ROWS, :]
            total = term if total is None else total + term
            product = grads[p, 0:ROWS, :] * x_ext[p, (2 - j) * NK : (2 - j) * NK + ROWS, :]
            small[pl.ds((TAP + 3 * p + j) * 8, 8), :] = jnp.sum(
                product.reshape(ROWS // 8, 8, 128), axis=0
            )
        raw[p * ROWS : (p + 1) * ROWS, :] = total
    small[pl.ds((TAP + 9) * 8, 56), :] = jnp.zeros((56, 128), F32)
    total = small[pl.ds(0, 48, stride=8), :]
    for s in range(1, 8):
        total = total + small[pl.ds(s, 48, stride=8), :]
    total = total + pltpu.roll(total, 64, 1)
    total = total + pltpu.roll(total, 32, 1)
    high = total.astype(BF16).astype(F32)
    low = total - high
    group = lane_group((24, 128))
    packed[0:24, :] = jnp.where(
        group == 0,
        high[0:24],
        jnp.where(group == 1, low[0:24], jnp.where(group == 2, high[24:48], low[24:48])),
    )
    packed[24:32, :] = jnp.zeros((8, 128), F32)
    for k in range(NK):
        for p in range(3):
            o_ref[k, p * STEPS : (p + 1) * STEPS, :] = raw[
                pl.ds(p * ROWS + k, STEPS, stride=NK), :
            ].astype(BF16)
        o_ref[k, 96:128, :] = packed[...].astype(BF16)


def unpack_kernel(x_ref, gp_ref, short_ref, res_ref, rate_ref, small):
    group = lane_group((32, 128))
    for g in range(4):
        columns = slice(g * 128, (g + 1) * 128)
        for p in range(3):
            parts = [x_ref[4 * g + r, p * STEPS : (p + 1) * STEPS, :].astype(F32) for r in range(4)]
            for q, out in enumerate(swap4(parts)):
                gp_ref[p, q * STEPS : (q + 1) * STEPS, columns] = out.astype(BF16)
        first = second = jnp.zeros((32, 128), F32)
        for r in range(4):
            pair = x_ref[4 * g + r, 96:128, :].astype(F32)
            pair = pair + pltpu.roll(pair, 96, 1)
            one = pair if r == 0 else pltpu.roll(pair, SUB * r, 1)
            two = pair if r == 2 else pltpu.roll(pair, (SUB * (r - 2)) % 128, 1)
            first = jnp.where(group == r, one, first)
            second = jnp.where(group == r, two, second)
        small[0:24, columns] = first[0:24]
        small[24:48, columns] = second[0:24]
    res_ref[...] = small[RES : RES + NM, :]
    rate_ref[...] = small[RATE : RATE + NM, :]
    for p in range(3):
        short_ref[p] = small[TAP + 3 * p : TAP + 3 * p + 3, :]


def weight_kernel(at_ref, rows1_ref, rows2_ref, y0, r1, r2, r3, r4, l3, l2, l1, own_ref, send_ref, y_all, y):
    z, h, spot = at_ref[0], at_ref[1], at_ref[3]
    for back, y_ref in enumerate((y0, r1, r2, r3, r4, l3, l2, l1)):
        y_all[(z - back + 8) % 8] = y_ref[...]
    for b, batch in enumerate(BATCHES):
        for i, away in enumerate(batch):
            k = shard_of(z, spot, away)
            for g in range(4):
                parts = [
                    y_all[2 * g + r // 2, jnp.bitwise_xor(r % 2, h), k].astype(F32)
                    for r in range(4)
                ]
                for q, out in enumerate(swap4(parts)):
                    first = b * 512 + i * 128 + q * STEPS
                    y[first : first + STEPS, g * 128 : (g + 1) * 128] = out.astype(BF16)
    over_rows = (((0,), (0,)), ((), ()))
    for x, out_ref in enumerate((own_ref, send_ref)):
        total = lax.dot_general(rows1_ref[x], y[0:512, :], over_rows, preferred_element_type=F32)
        total += lax.dot_general(
            rows2_ref[x], y[512:1024, :], over_rows, preferred_element_type=F32
        )
        out_ref[...] = total.astype(out_ref.dtype)


def shape(dims, dtype=F32):
    return jax.ShapeDtypeStruct(dims, dtype)


def sent(dims):
    return pltpu.HBM(dims, BF16)


def scratch(*dims):
    return pltpu.VMEM(dims, F32)


SCANS = [
    scratch(NK * 96, 128),
    scratch(3, ROWS + 2 * NK, 128),
    scratch(3, ROWS, 128),
    scratch(ROWS, 128),
    scratch(NM * NK, 128),
    scratch(NM * NK, 128),
]


def call(kernel, **settings):
    def run(*args):
        return pl.pallas_call(kernel, **settings)(*args)

    return run


def compute(out_grad, out_weight, projections, short_filters, residues, decay_rates):
    z, h, xl, spot_y, core = (lax.axis_index(a) for a in CTX + FSDP)
    here = jnp.stack([z, h, core, 4 * xl + spot_y, 2 * z + h]).astype(jnp.int32)

    route = [
        (zz * 8 + at, at * 8 + (at - zz) % 8) for zz in range(8) for at in range(8)
    ]
    moved = lax.ppermute(out_grad, ("z", "xl", "y"), route)

    def flip(value, axis, by):
        return lax.ppermute(value, axis, [(i, i ^ by) for i in range(lax.axis_size(axis))])

    across = flip(moved, "xl", 1)
    near, wrap = flip(moved, "y", 1), flip(moved, "y", 3)
    near2, wrap2 = flip(across, "y", 1), flip(across, "y", 3)
    far, far2 = flip(wrap, "y", 1), flip(near2, "y", 3)
    mine1 = jnp.stack([moved, across, near, wrap])
    mine2 = jnp.stack([near2, wrap2, far, far2])
    theirs1, theirs2 = flip(mine1, "core", 1), flip(mine2, "core", 1)
    other_weight = flip(out_weight, "xh", 1)

    chunks, prm = call(
        pack_kernel,
        out_shape=(sent((NK, 96, 128)), shape((56, 128))),
        in_specs=[pl.BlockSpec(memory_space=pltpu.SMEM)] + [VMEM] * 4,
        out_specs=(pl.BlockSpec(), VMEM),
    )(here[4:], projections, residues, decay_rates, short_filters)
    x = lax.all_to_all(chunks, CTX, 0, 0)

    smem = pl.BlockSpec(memory_space=pltpu.SMEM)
    keep, send, state_in = call(
        forward_kernel,
        out_shape=(shape((8, STEPS, 128), BF16), shape((8, STEPS, 128), BF16), shape((NM * NK, 128))),
        in_specs=[smem, VMEM, VMEM],
        out_specs=(VMEM,) * 3,
        scratch_shapes=SCANS + [scratch(ROWS, 128)],
        compiler_params=PARAMS,
    )(here, x, prm)

    def turn(value, by):
        return lax.ppermute(value, "z", [(i, (i + by) % 8) for i in range(8)])

    y0 = jnp.stack([keep, flip(send, "xh", 1)])
    r1, l1 = turn(y0, 1), turn(y0, -1)
    r2, l2 = turn(r1, 1), turn(l1, -1)
    r3, l3 = turn(r2, 1), turn(l2, -1)
    r4 = turn(r2, 2)

    grads, rows, after = [], [], state_in
    for mine, theirs in ((mine1, theirs1), (mine2, theirs2)):
        parts, blocks = call(
            partial_kernel,
            out_shape=(sent((NK, 4, STEPS, 128)), sent((2, 512, 512))),
            in_specs=[smem] + [VMEM] * 4 + [pl.BlockSpec(memory_space=pl.ANY)],
            out_specs=(pl.BlockSpec(), pl.BlockSpec()),
            compiler_params=PARAMS,
        )(here, mine, theirs, out_weight, other_weight, after)
        grads.append(lax.all_to_all(parts, CTX, 0, 0))
        rows.append(blocks)

    out = call(
        backward_kernel,
        out_shape=sent((NK, 128, 128)),
        in_specs=[smem] + [VMEM] * 5,
        out_specs=pl.BlockSpec(),
        scratch_shapes=SCANS
        + [scratch(ROWS, 128)] * 3
        + [scratch(NM, ROWS + NK, 128), scratch(ROWS, 128), scratch(3, ROWS + 2 * NK, 128)]
        + [scratch(3 * ROWS, 128), scratch(48 * 8, 128), scratch(32, 128)],
        compiler_params=PARAMS,
    )(here, x, prm, state_in, *grads)
    back = lax.all_to_all(out, CTX, 0, 0)
    grad_projections, grad_short, grad_res, grad_rate = call(
        unpack_kernel,
        out_shape=(shape((3, 128, 512), BF16), shape((3, 3, 512)), shape((NM, 512)), shape((NM, 512))),
        in_specs=[VMEM],
        out_specs=(VMEM,) * 4,
        scratch_shapes=[scratch(48, 512)],
    )(back)

    own, send = call(
        weight_kernel,
        out_shape=(shape((512, 512)), shape((512, 512), BF16)),
        in_specs=[smem] + [VMEM] * 10,
        out_specs=(VMEM, VMEM),
        scratch_shapes=[pltpu.VMEM((8, 2, 8, STEPS, 128), BF16), pltpu.VMEM((1024, 512), BF16)],
        compiler_params=PARAMS,
    )(here, *rows, y0, r1, r2, r3, r4, l3, l2, l1)
    grad_weight = (own + flip(send, "xh", 1).astype(F32)).astype(BF16)
    return grad_weight, grad_projections, grad_short, grad_res, grad_rate


def solution(mesh):
    fine = Mesh(mesh.devices.reshape(8, 2, 2, 4, 2), CTX + FSDP)
    placed = (
        P(CTX, FSDP),
        P(CTX, FSDP),
        P(None, CTX, FSDP),
        P(None, None, FSDP),
        P(None, FSDP),
        P(None, FSDP),
    )
    return jax.shard_map(
        compute,
        mesh=fine,
        in_specs=placed,
        out_specs=(
            P(CTX, FSDP),
            P(None, CTX, FSDP),
            P(None, None, FSDP),
            P(None, FSDP),
            P(None, FSDP),
        ),
        check_vma=False,
    )
```

```python
import jax
import jax.numpy as jnp
from jax import lax
from jax.experimental import pallas as pl
from jax.experimental.pallas import tpu as pltpu
from jax.sharding import Mesh
from jax.sharding import PartitionSpec as P


F32 = jnp.float32
BF16 = jnp.bfloat16
CTX = ("z", "xh")
FSDP = ("xl", "y", "core")
SUB = 32
NM = 16
STEPS = 32
NK = 16
ROWS = STEPS * NK
VMEM = pl.BlockSpec(memory_space=pltpu.VMEM)
RES, RATE, TAP = 0, 16, 32
PARAMS = pltpu.CompilerParams(vmem_limit_bytes=48 * 2**20)


def lane_group(shape):
    return lax.broadcasted_iota(jnp.int32, shape, len(shape) - 1) // SUB


def swap4(parts):
    group = lane_group(parts[0].shape)
    outs = []
    for r in range(4):
        total = None
        for q in range(4):
            turn = (SUB * (q - r)) % 128
            moved = parts[q] if turn == 0 else pltpu.roll(parts[q], turn, 1)
            total = moved if total is None else jnp.where(group == q, moved, total)
        outs.append(total)
    return outs


def shift_blocks(values, blocks, reverse=False):
    rows = values.shape[0]
    row = lax.broadcasted_iota(jnp.int32, values.shape, 0) % NK
    group = lane_group(values.shape)
    if blocks >= 4:
        by = blocks // 4
        if reverse:
            return jnp.where(row < NK - by, pltpu.roll(values, rows - by, 0), 0.0)
        return jnp.where(row >= by, pltpu.roll(values, by, 0), 0.0)
    if reverse:
        turned = pltpu.roll(values, 128 - SUB * blocks, 1)
        over = jnp.where(row < NK - 1, pltpu.roll(turned, rows - 1, 0), 0.0)
        return jnp.where(group >= 4 - blocks, over, turned)
    turned = pltpu.roll(values, SUB * blocks, 1)
    over = jnp.where(row >= 1, pltpu.roll(turned, 1, 0), 0.0)
    return jnp.where(group < blocks, over, turned)


def pack_kernel(at_ref, x_ref, res_ref, rate_ref, tap_ref, o_ref, prm_ref):
    for p in range(3):
        for g in range(4):
            parts = [
                x_ref[p, q * STEPS : (q + 1) * STEPS, g * 128 : (g + 1) * 128].astype(F32)
                for q in range(4)
            ]
            for r, out in enumerate(swap4(parts)):
                o_ref[4 * g + r, p * STEPS : (p + 1) * STEPS, :] = out.astype(BF16)
    m = at_ref[0]
    columns = pl.ds(pl.multiple_of(m // 4 * 128, 128), 128)

    def own(values):
        values = pltpu.roll(values, (4 - m % 4) % 4 * SUB, 1)
        values = jnp.where(lane_group(values.shape) == 0, values, 0.0)
        values = values + pltpu.roll(values, 64, 1)
        return values + pltpu.roll(values, 32, 1)

    prm_ref[RES : RES + NM, :] = own(res_ref[:, columns])
    prm_ref[RATE : RATE + NM, :] = own(rate_ref[:, columns])
    for p in range(3):
        prm_ref[TAP + 8 * p : TAP + 8 * p + 3, :] = own(tap_ref[p, :, columns])


def prepare(x_ref, prm_ref, wide, x_ext, branch):
    wide[...] = x_ref[...].reshape(NK * 96, 128).astype(F32)
    for p in range(3):
        for t in range(STEPS):
            x_ext[p, (t + 2) * NK : (t + 3) * NK, :] = wide[pl.ds(p * STEPS + t, NK, stride=96), :]
        for back in range(2):
            x_ext[p, back * NK : (back + 1) * NK, :] = shift_blocks(
                x_ext[p, (STEPS + back) * NK : (STEPS + back + 1) * NK, :], 1
            )
        total = None
        for j in range(3):
            tap = prm_ref[TAP + 8 * p + j : TAP + 8 * p + j + 1, :]
            term = tap * x_ext[p, (2 - j) * NK : (2 - j) * NK + ROWS, :]
            total = term if total is None else total + term
        branch[p] = total


def spread(prm_ref, first, out):
    for n in range(NM):
        out[n * NK : (n + 1) * NK, :] = jnp.broadcast_to(
            prm_ref[first + n : first + n + 1, :], (NK, 128)
        )


def ends(source, decay8, out, reverse):
    for v in range(2):

        def step(i, state):
            t = STEPS - 1 - i if reverse else i
            value = source[pl.ds(pl.multiple_of(t * NK + v * 8, 8), 8), :]
            return tuple(decay8[n] * state[n] + value for n in range(NM))

        state = lax.fori_loop(
            0, STEPS, step, tuple(jnp.zeros((8, 128), F32) for _ in range(NM)), unroll=8
        )
        for n in range(NM):
            out[n * NK + v * 8 : n * NK + v * 8 + 8, :] = state[n]


def entering(ends_ref, rates, reverse):
    total = ends_ref[...]
    for log in range(6):
        blocks = 2**log
        power = jnp.exp(rates[...] * (-float(STEPS * blocks)))
        total = total + power * shift_blocks(total, blocks, reverse)
    return shift_blocks(total, 1, reverse)


def decays(prm_ref):
    return [
        jnp.exp(-jnp.broadcast_to(prm_ref[RATE + n : RATE + n + 1, :], (8, 128)))
        for n in range(NM)
    ]


def weights(prm_ref):
    return [jnp.broadcast_to(prm_ref[RES + n : RES + n + 1, :], (8, 128)) for n in range(NM)]


def forward_kernel(at_ref, x_ref, prm_ref, keep_ref, send_ref, in_ref, wide, x_ext, branch, kv, rates, tails, y):
    prepare(x_ref, prm_ref, wide, x_ext, branch)
    kv[...] = branch[1] * branch[2]
    spread(prm_ref, RATE, rates)
    decay8 = decays(prm_ref)
    ends(kv, decay8, tails, False)
    in_ref[...] = entering(tails, rates, False)
    weight8 = weights(prm_ref)
    for v in range(2):

        def step(t, state):
            at = pl.ds(pl.multiple_of(t * NK + v * 8, 8), 8)
            value = kv[at, :]
            state = tuple(decay8[n] * state[n] + value for n in range(NM))
            terms = [weight8[n] * state[n] for n in range(NM)]
            while len(terms) > 1:
                terms = [a + b for a, b in zip(terms[::2], terms[1::2])]
            y[at, :] = branch[0, at, :] * terms[0]
            return state

        lax.fori_loop(
            0,
            STEPS,
            step,
            tuple(in_ref[n * NK + v * 8 : n * NK + v * 8 + 8, :] for n in range(NM)),
            unroll=4,
        )
    h = at_ref[1]
    for k in range(8):
        keep_ref[k] = y[pl.ds(2 * k + h, STEPS, stride=NK), :].astype(BF16)
        send_ref[k] = y[pl.ds(2 * k + 1 - h, STEPS, stride=NK), :].astype(BF16)


BATCHES = ((0, 4, 1, 3), (5, 7, 2, 6))


def shard_of(z, spot, away):
    return (z - jnp.bitwise_xor(spot, away) + 8) % 8


def partial_kernel(at_ref, mine_ref, theirs_ref, w0_ref, w1_ref, after_ref, o_ref, rows_ref):
    own_first = at_ref[1] == at_ref[2]
    for i in range(4):
        mine, theirs = mine_ref[i], theirs_ref[i]
        rows_ref[0, i * 128 : (i + 1) * 128, :] = jnp.where(own_first, mine, theirs)
        rows_ref[1, i * 128 : (i + 1) * 128, :] = jnp.where(own_first, theirs, mine)
    for i in range(4):
        total = jnp.dot(
            rows_ref[0, i * 128 : (i + 1) * 128, :], w0_ref[...], preferred_element_type=F32
        ) + jnp.dot(
            rows_ref[1, i * 128 : (i + 1) * 128, :], w1_ref[...], preferred_element_type=F32
        )
        for g in range(4):
            parts = [total[q * STEPS : (q + 1) * STEPS, g * 128 : (g + 1) * 128] for q in range(4)]
            for r, out in enumerate(swap4(parts)):
                o_ref[4 * g + r, i] = out.astype(BF16)


def backward_kernel(at_ref, x_ref, prm_ref, in_ref, gy1_ref, gy2_ref, o_ref, wide, x_ext, branch, kv, rates, tails, gy, gl, long_out, states, gkv, grads, raw, small, packed):
    prepare(x_ref, prm_ref, wide, x_ext, branch)
    kv[...] = branch[1] * branch[2]
    spread(prm_ref, RATE, rates)
    decay8 = decays(prm_ref)
    weight8 = weights(prm_ref)
    for n in range(NM):
        states[n, 0:NK, :] = in_ref[n * NK : (n + 1) * NK, :]
    for v in range(2):

        def forward(t, state):
            at = pl.ds(pl.multiple_of(t * NK + v * 8, 8), 8)
            value = kv[at, :]
            state = tuple(decay8[n] * state[n] + value for n in range(NM))
            later = pl.ds(pl.multiple_of((t + 1) * NK + v * 8, 8), 8)
            for n in range(NM):
                states[n, later, :] = state[n]
            terms = [weight8[n] * state[n] for n in range(NM)]
            while len(terms) > 1:
                terms = [a + b for a, b in zip(terms[::2], terms[1::2])]
            long_out[at, :] = terms[0]
            return state

        lax.fori_loop(
            0,
            STEPS,
            forward,
            tuple(in_ref[n * NK + v * 8 : n * NK + v * 8 + 8, :] for n in range(NM)),
            unroll=4,
        )
    spot = at_ref[3]
    wide[0:ROWS, :] = jnp.zeros((ROWS, 128), F32)
    for batch, gy_ref in zip(BATCHES, (gy1_ref, gy2_ref)):
        for i, away in enumerate(batch):
            for source in range(NK):
                k = 2 * shard_of(source // 2, spot, away) + source % 2
                at = pl.ds(pl.multiple_of(k * STEPS, STEPS), STEPS)
                wide[at, :] = wide[at, :] + gy_ref[source, i].astype(F32)
    for t in range(STEPS):
        gy[t * NK : (t + 1) * NK, :] = wide[pl.ds(t, NK, stride=STEPS), :]
    gl[...] = gy[...] * branch[0]
    grads[0, 0:ROWS, :] = gy[...] * long_out[...]
    ends(gl, decay8, tails, True)
    tails[...] = entering(tails, rates, True)
    zero = jnp.zeros((8, 128), F32)
    for half in range(2):
        modes = range(half * 8, half * 8 + 8)
        decay = [jnp.exp(-jnp.broadcast_to(prm_ref[RATE + n : RATE + n + 1, :], (8, 128))) for n in modes]
        weight = [jnp.broadcast_to(prm_ref[RES + n : RES + n + 1, :], (8, 128)) for n in modes]
        for v in range(2):

            def backward(i, carry):
                adjoint, by_res, by_rate = carry
                t = STEPS - 1 - i
                at = pl.ds(pl.multiple_of(t * NK + v * 8, 8), 8)
                later = pl.ds(pl.multiple_of((t + 1) * NK + v * 8, 8), 8)
                value = gl[at, :]
                adjoint = tuple(decay[m] * adjoint[m] + value for m in range(8))
                by_res = tuple(by_res[m] + value * states[n, later, :] for m, n in enumerate(modes))
                by_rate = tuple(
                    by_rate[m] + adjoint[m] * states[n, at, :] for m, n in enumerate(modes)
                )
                terms = [weight[m] * adjoint[m] for m in range(8)]
                while len(terms) > 1:
                    terms = [a + b for a, b in zip(terms[::2], terms[1::2])]
                if half == 0:
                    gkv[at, :] = terms[0]
                else:
                    gkv[at, :] = gkv[at, :] + terms[0]
                return adjoint, by_res, by_rate

            zeros = tuple(zero for _ in range(8))
            first = tuple(tails[n * NK + v * 8 : n * NK + v * 8 + 8, :] for n in modes)
            _, by_res, by_rate = lax.fori_loop(0, STEPS, backward, (first, zeros, zeros), unroll=4)
            for m, n in enumerate(modes):
                rate_part = by_rate[m] * (-decay[m] * weight[m])
                to_res = pl.ds((RES + n) * 8, 8)
                to_rate = pl.ds((RATE + n) * 8, 8)
                if v == 0:
                    small[to_res, :] = by_res[m]
                    small[to_rate, :] = rate_part
                else:
                    small[to_res, :] = small[to_res, :] + by_res[m]
                    small[to_rate, :] = small[to_rate, :] + rate_part
    grads[1, 0:ROWS, :] = gkv[...] * branch[2]
    grads[2, 0:ROWS, :] = gkv[...] * branch[1]
    for p in range(3):
        for ahead in range(2):
            grads[p, ROWS + ahead * NK : ROWS + (ahead + 1) * NK, :] = shift_blocks(
                grads[p, ahead * NK : (ahead + 1) * NK, :], 1, True
            )
        total = None
        for j in range(3):
            tap = prm_ref[TAP + 8 * p + j : TAP + 8 * p + j + 1, :]
            term = tap * grads[p, j * NK : j * NK + ROWS, :]
            total = term if total is None else total + term
            product = grads[p, 0:ROWS, :] * x_ext[p, (2 - j) * NK : (2 - j) * NK + ROWS, :]
            small[pl.ds((TAP + 3 * p + j) * 8, 8), :] = jnp.sum(
                product.reshape(ROWS // 8, 8, 128), axis=0
            )
        raw[p * ROWS : (p + 1) * ROWS, :] = total
    small[pl.ds((TAP + 9) * 8, 56), :] = jnp.zeros((56, 128), F32)
    total = small[pl.ds(0, 48, stride=8), :]
    for s in range(1, 8):
        total = total + small[pl.ds(s, 48, stride=8), :]
    total = total + pltpu.roll(total, 64, 1)
    total = total + pltpu.roll(total, 32, 1)
    high = total.astype(BF16).astype(F32)
    low = total - high
    group = lane_group((24, 128))
    packed[0:24, :] = jnp.where(
        group == 0,
        high[0:24],
        jnp.where(group == 1, low[0:24], jnp.where(group == 2, high[24:48], low[24:48])),
    )
    packed[24:32, :] = jnp.zeros((8, 128), F32)
    for k in range(NK):
        for p in range(3):
            o_ref[k, p * STEPS : (p + 1) * STEPS, :] = raw[
                pl.ds(p * ROWS + k, STEPS, stride=NK), :
            ].astype(BF16)
        o_ref[k, 96:128, :] = packed[...].astype(BF16)


def unpack_kernel(x_ref, gp_ref, short_ref, res_ref, rate_ref, small):
    group = lane_group((32, 128))
    for g in range(4):
        columns = slice(g * 128, (g + 1) * 128)
        for p in range(3):
            parts = [x_ref[4 * g + r, p * STEPS : (p + 1) * STEPS, :].astype(F32) for r in range(4)]
            for q, out in enumerate(swap4(parts)):
                gp_ref[p, q * STEPS : (q + 1) * STEPS, columns] = out.astype(BF16)
        first = second = jnp.zeros((32, 128), F32)
        for r in range(4):
            pair = x_ref[4 * g + r, 96:128, :].astype(F32)
            pair = pair + pltpu.roll(pair, 96, 1)
            one = pair if r == 0 else pltpu.roll(pair, SUB * r, 1)
            two = pair if r == 2 else pltpu.roll(pair, (SUB * (r - 2)) % 128, 1)
            first = jnp.where(group == r, one, first)
            second = jnp.where(group == r, two, second)
        small[0:24, columns] = first[0:24]
        small[24:48, columns] = second[0:24]
    res_ref[...] = small[RES : RES + NM, :]
    rate_ref[...] = small[RATE : RATE + NM, :]
    for p in range(3):
        short_ref[p] = small[TAP + 3 * p : TAP + 3 * p + 3, :]


def weight_kernel(at_ref, rows1_ref, rows2_ref, y0, r1, r2, r3, r4, l3, l2, l1, own_ref, send_ref, y_all, y):
    z, h, spot = at_ref[0], at_ref[1], at_ref[3]
    for back, y_ref in enumerate((y0, r1, r2, r3, r4, l3, l2, l1)):
        y_all[(z - back + 8) % 8] = y_ref[...]
    for b, batch in enumerate(BATCHES):
        for i, away in enumerate(batch):
            k = shard_of(z, spot, away)
            for g in range(4):
                parts = [
                    y_all[2 * g + r // 2, jnp.bitwise_xor(r % 2, h), k].astype(F32)
                    for r in range(4)
                ]
                for q, out in enumerate(swap4(parts)):
                    first = b * 512 + i * 128 + q * STEPS
                    y[first : first + STEPS, g * 128 : (g + 1) * 128] = out.astype(BF16)
    over_rows = (((0,), (0,)), ((), ()))
    for x, out_ref in enumerate((own_ref, send_ref)):
        total = lax.dot_general(rows1_ref[x], y[0:512, :], over_rows, preferred_element_type=F32)
        total += lax.dot_general(
            rows2_ref[x], y[512:1024, :], over_rows, preferred_element_type=F32
        )
        out_ref[...] = total.astype(out_ref.dtype)


def shape(dims, dtype=F32):
    return jax.ShapeDtypeStruct(dims, dtype)


def sent(dims):
    return pltpu.HBM(dims, BF16)


def scratch(*dims):
    return pltpu.VMEM(dims, F32)


SCANS = [
    scratch(NK * 96, 128),
    scratch(3, ROWS + 2 * NK, 128),
    scratch(3, ROWS, 128),
    scratch(ROWS, 128),
    scratch(NM * NK, 128),
    scratch(NM * NK, 128),
]


def call(kernel, **settings):
    def run(*args):
        return pl.pallas_call(kernel, **settings)(*args)

    return run


def compute(out_grad, out_weight, projections, short_filters, residues, decay_rates):
    z, h, xl, spot_y, core = (lax.axis_index(a) for a in CTX + FSDP)
    here = jnp.stack([z, h, core, 4 * xl + spot_y, 2 * z + h]).astype(jnp.int32)

    route = [
        (zz * 8 + at, at * 8 + (at - zz) % 8) for zz in range(8) for at in range(8)
    ]
    moved = lax.ppermute(out_grad, ("z", "xl", "y"), route)

    def flip(value, axis, by):
        return lax.ppermute(value, axis, [(i, i ^ by) for i in range(lax.axis_size(axis))])

    across = flip(moved, "xl", 1)
    near, wrap = flip(moved, "y", 1), flip(moved, "y", 3)
    near2, wrap2 = flip(across, "y", 1), flip(across, "y", 3)
    far, far2 = flip(wrap, "y", 1), flip(near2, "y", 3)
    mine1 = jnp.stack([moved, across, near, wrap])
    mine2 = jnp.stack([near2, wrap2, far, far2])
    theirs1, theirs2 = flip(mine1, "core", 1), flip(mine2, "core", 1)
    other_weight = flip(out_weight, "xh", 1)

    chunks, prm = call(
        pack_kernel,
        out_shape=(sent((NK, 96, 128)), shape((56, 128))),
        in_specs=[pl.BlockSpec(memory_space=pltpu.SMEM)] + [VMEM] * 4,
        out_specs=(pl.BlockSpec(), VMEM),
    )(here[4:], projections, residues, decay_rates, short_filters)
    x = lax.all_to_all(chunks, CTX, 0, 0)

    smem = pl.BlockSpec(memory_space=pltpu.SMEM)
    keep, send, state_in = call(
        forward_kernel,
        out_shape=(shape((8, STEPS, 128), BF16), shape((8, STEPS, 128), BF16), shape((NM * NK, 128))),
        in_specs=[smem, VMEM, VMEM],
        out_specs=(VMEM,) * 3,
        scratch_shapes=SCANS + [scratch(ROWS, 128)],
        compiler_params=PARAMS,
    )(here, x, prm)

    def turn(value, by):
        return lax.ppermute(value, "z", [(i, (i + by) % 8) for i in range(8)])

    y0 = jnp.stack([keep, flip(send, "xh", 1)])
    r1, l1 = turn(y0, 1), turn(y0, -1)
    r2, l2 = turn(r1, 1), turn(l1, -1)
    r3, l3 = turn(r2, 1), turn(l2, -1)
    r4 = turn(r2, 2)

    grads, rows, after = [], [], state_in
    for mine, theirs in ((mine1, theirs1), (mine2, theirs2)):
        parts, blocks = call(
            partial_kernel,
            out_shape=(sent((NK, 4, STEPS, 128)), sent((2, 512, 512))),
            in_specs=[smem] + [VMEM] * 4 + [pl.BlockSpec(memory_space=pl.ANY)],
            out_specs=(pl.BlockSpec(), pl.BlockSpec()),
            compiler_params=PARAMS,
        )(here, mine, theirs, out_weight, other_weight, after)
        grads.append(lax.all_to_all(parts, CTX, 0, 0))
        rows.append(blocks)

    out = call(
        backward_kernel,
        out_shape=sent((NK, 128, 128)),
        in_specs=[smem] + [VMEM] * 5,
        out_specs=pl.BlockSpec(),
        scratch_shapes=SCANS
        + [scratch(ROWS, 128)] * 3
        + [scratch(NM, ROWS + NK, 128), scratch(ROWS, 128), scratch(3, ROWS + 2 * NK, 128)]
        + [scratch(3 * ROWS, 128), scratch(48 * 8, 128), scratch(32, 128)],
        compiler_params=PARAMS,
    )(here, x, prm, state_in, *grads)
    back = lax.all_to_all(out, CTX, 0, 0)
    grad_projections, grad_short, grad_res, grad_rate = call(
        unpack_kernel,
        out_shape=(shape((3, 128, 512), BF16), shape((3, 3, 512)), shape((NM, 512)), shape((NM, 512))),
        in_specs=[VMEM],
        out_specs=(VMEM,) * 4,
        scratch_shapes=[scratch(48, 512)],
    )(back)

    own, send = call(
        weight_kernel,
        out_shape=(shape((512, 512)), shape((512, 512), BF16)),
        in_specs=[smem] + [VMEM] * 10,
        out_specs=(VMEM, VMEM),
        scratch_shapes=[pltpu.VMEM((8, 2, 8, STEPS, 128), BF16), pltpu.VMEM((1024, 512), BF16)],
        compiler_params=PARAMS,
    )(here, *rows, y0, r1, r2, r3, r4, l3, l2, l1)
    grad_weight = (own + flip(send, "xh", 1).astype(F32)).astype(BF16)
    return grad_weight, grad_projections, grad_short, grad_res, grad_rate


def solution(mesh):
    fine = Mesh(mesh.devices.reshape(8, 2, 2, 4, 2), CTX + FSDP)
    placed = (
        P(CTX, FSDP),
        P(CTX, FSDP),
        P(None, CTX, FSDP),
        P(None, None, FSDP),
        P(None, FSDP),
        P(None, FSDP),
    )
    return jax.shard_map(
        compute,
        mesh=fine,
        in_specs=placed,
        out_specs=(
            P(CTX, FSDP),
            P(None, CTX, FSDP),
            P(None, None, FSDP),
            P(None, FSDP),
            P(None, FSDP),
        ),
        check_vma=False,
    )
```
